32 devices in a mesh: seq: 16 (over z, x, core), fsdp: 2 (over y).
Axes of the slice: x: 2, y: 2, z: 4, core: 2. Of those that a mesh axis runs over, the one named last changes fastest.
Arguments:
- inputs: bfloat16 [2, 16384, 1024], P(None, 'seq', 'fsdp'), may hold values from -6 to 6
- first_factor: bfloat16 [128, 128, 128], P('seq'), may hold values from -0.5 to 0.5
- second_factor: bfloat16 [128, 128, 128], P('seq'), may hold values from -0.5 to 0.5
- gate_scale: float32 [1024], P('fsdp'), may hold values from -2 to 2
- gate_bias: float32 [1024], P('fsdp'), may hold values from -3 to 3
- in_weight: bfloat16 [1024, 4096], P('seq', 'fsdp'), may hold values from -0.1875 to 0.1875
- out_weight: bfloat16 [4096, 1024], P('fsdp', 'seq'), may hold values from -0.09375 to 0.09375
- cotangent: bfloat16 [2, 16384, 1024], P(None, 'seq', 'fsdp'), may hold values from -6 to 6
Outputs:
- result: bfloat16 [2, 16384, 1024], P(None, 'seq', 'fsdp')
- input_grad: bfloat16 [2, 16384, 1024], P(None, 'seq', 'fsdp')
- grad_in: float32 [1024, 4096], P('seq', 'fsdp')
- grad_out: float32 [4096, 1024], P('fsdp', 'seq')
The draws below stay inside these ranges and needn't reach their ends.
All inputs are finite; a program needn't handle non-finite values.
Results may differ from the reference program's by a relative error of at most 0.0075.
Values may be sent and summed in bfloat16 or wider, within the bound.
A program may use at most 192 MiB of HBM per device.

```python
import jax
import jax.numpy as jnp
from jax import lax

CH = 1024
FF = 4096
NB = 128
BS = 128
NSEQ = 2
SEQLEN = 16384


def with_spikes(array, rng, source, target, blocks, factor):
    owner, partner = [(jnp.arange(array.shape[position]) // (array.shape[position] // blocks)).reshape([-1 if axis == position else 1 for axis in range(array.ndim)]) for position in (source, target)]
    chosen = jax.random.permutation(rng, blocks)[partner]
    strong = (owner == chosen) | (owner == (partner + blocks // 2) % blocks)
    return jnp.where(strong, factor * array, array)


def level_of(key, extent, shards, least, high):
    def one(dim, blocks):
        draws = jax.random.uniform(jax.random.fold_in(jax.random.fold_in(key, 6), dim), (blocks,), jnp.float32, least / len(shards), high / len(shards))
        return jnp.repeat(jnp.exp(draws), extent[dim] // blocks).reshape((-1,) + (1,) * (len(extent) - dim - 1))

    level = one(*shards[0])
    for cut in shards[1:]:
        level = level * one(*cut)
    return level


def centred(rng, shape, deviation, bound, pieces=(), held_as=jnp.bfloat16):
    values = jax.random.normal(rng, shape, jnp.float32) * deviation
    if len(pieces) > 0:
        values = level_of(rng, shape, pieces, -0.22, 0.18) * values
    return jnp.clip(values, min=-bound, max=bound).astype(held_as)


def heavy_noise(key, extent, scale, reach, shards, heavy, dtype=jnp.bfloat16):
    values = scale * jax.random.normal(key, extent, jnp.float32)
    if shards:
        values = values * level_of(key, extent, shards, -0.22, 0.18)
    return jnp.clip(with_spikes(values, jax.random.fold_in(key, 3), *heavy), -reach, reach).astype(dtype)


def setup_inputs(seed: int = 0) -> dict:
    splits = jax.random.split(jax.random.key(seed), 9)
    return {
        "inputs": centred(splits[0], (NSEQ, SEQLEN, CH), 1.0, 6.0, ((1, 16), (2, 2))),
        "first_factor": centred(splits[1], (NB, BS, BS), BS ** -0.5, 0.5, ((0, 16),)),
        "second_factor": centred(splits[2], (BS, NB, NB), NB ** -0.5, 0.5, ((0, 16),)),
        "gate_scale": jnp.clip(jax.random.uniform(splits[3], (CH,), jnp.float32, -2.0, 2.0) * level_of(splits[3], (CH,), ((0, 2),), -0.4, 0.0), -2.0, 2.0),
        "gate_bias": centred(splits[4], (CH,), 0.7, 3.0, ((0, 2),), jnp.float32),
        "in_weight": centred(splits[5], (CH, FF), CH ** -0.5, 0.1875, ((0, 16), (1, 2))),
        "out_weight": centred(splits[6], (FF, CH), FF ** -0.5, 0.09375, ((0, 2), (1, 16))),
        "cotangent": heavy_noise(splits[7], (NSEQ, SEQLEN, CH), 1.0, 6.0, ((1, 16), (2, 2)), (1, 2, 16, 2.0)),
    }


def reference(inputs, first_factor, second_factor, gate_scale, gate_bias, in_weight, out_weight, cotangent):
    factor_one = first_factor.astype(jnp.float32)
    factor_two = second_factor.astype(jnp.float32)

    def one_sequence(carry, pair):
        source, upstream = pair
        grid = source.reshape(NB, BS, CH)
        section_one = jnp.einsum("mkn,mnc->mkc", factor_one, grid.astype(jnp.float32)).astype(jnp.bfloat16)
        section_two = jnp.einsum("kjm,mkc->jkc", factor_two, section_one.astype(jnp.float32)).astype(jnp.bfloat16)
        section_two = lax.optimization_barrier(section_two)
        gate = jax.nn.sigmoid(gate_scale * grid.astype(jnp.float32) + gate_bias)
        mixed = (gate * section_two.astype(jnp.float32)).astype(jnp.bfloat16).reshape(SEQLEN, CH)
        pre_act = jnp.dot(mixed, in_weight, preferred_element_type=jnp.float32)
        hidden = jax.nn.silu(pre_act).astype(jnp.bfloat16)
        result = (mixed.astype(jnp.float32) + jnp.dot(hidden, out_weight, preferred_element_type=jnp.float32)).astype(jnp.bfloat16)
        hidden_grad = jnp.dot(upstream, out_weight.T, preferred_element_type=jnp.float32)
        sigma = jax.nn.sigmoid(pre_act)
        pre_grad = (hidden_grad * sigma * (1.0 + pre_act * (1.0 - sigma))).astype(jnp.bfloat16)
        term_out = jnp.dot(hidden.T, upstream, preferred_element_type=jnp.float32)
        term_in = jnp.dot(mixed.T, pre_grad, preferred_element_type=jnp.float32)
        mixed_grad = (upstream.astype(jnp.float32) + jnp.dot(pre_grad, in_weight.T, preferred_element_type=jnp.float32)).astype(jnp.bfloat16)
        grad_grid = mixed_grad.reshape(NB, BS, CH).astype(jnp.float32)
        second_grad = (grad_grid * gate).astype(jnp.bfloat16)
        gate_back = grad_grid * section_two.astype(jnp.float32) * gate * (1.0 - gate) * gate_scale
        first_grad = jnp.einsum("kjm,jkc->mkc", factor_two, second_grad.astype(jnp.float32)).astype(jnp.bfloat16)
        input_grad = (jnp.einsum("mkn,mkc->mnc", factor_one, first_grad.astype(jnp.float32)) + gate_back).astype(jnp.bfloat16)
        return (carry[0] + term_in, carry[1] + term_out), (result, input_grad.reshape(SEQLEN, CH))

    start = (jnp.zeros((CH, FF), jnp.float32), jnp.zeros((FF, CH), jnp.float32))
    (sum_in, sum_out), (result, input_grad) = lax.scan(one_sequence, start, (inputs, cotangent))
    return result, input_grad, sum_in * (1.0 / BS), sum_out * (1.0 / BS)
```

```python
import jax
import jax.numpy as jnp
from jax import lax
from jax.sharding import PartitionSpec as P

BF = jnp.bfloat16
F32 = jnp.float32


def body(
    inputs, first_factor, second_factor, gate_scale, gate_bias, in_weight, out_weight, cotangent
):
    seq_count, tok_rows, chan = inputs.shape
    blocks, size, _ = first_factor.shape
    offs = second_factor.shape[0]
    owners = lax.axis_size("seq")
    groups = lax.axis_size("fsdp")
    mine = lax.axis_index("fsdp")
    width = chan * groups
    gain = gate_scale.reshape(1, 1, chan)
    shift = gate_bias.reshape(1, 1, chan)

    def swap(x):
        return lax.ppermute(x, "fsdp", [(0, 1), (1, 0)])

    def gather_cols(x):
        if groups != 2:
            return lax.all_gather(x, "fsdp", axis=1, tiled=True)
        y = swap(x)
        first = mine == 0
        return jnp.concatenate([jnp.where(first, x, y), jnp.where(first, y, x)], axis=1)

    def reduce_cols(left, weight, dims):
        if groups != 2:
            full = lax.dot_general(left, weight, dims, preferred_element_type=F32)
            got = lax.all_to_all(full, "fsdp", split_axis=1, concat_axis=0, tiled=True)
            return jnp.sum(got.reshape(groups, -1, chan), axis=0), None
        other = lax.dynamic_slice_in_dim(weight, (1 - mine) * chan, chan, 0)
        own = lax.dynamic_slice_in_dim(weight, mine * chan, chan, 0)
        sent = swap(lax.dot_general(left, other, dims, preferred_element_type=F32).astype(BF))
        kept = lax.dot_general(left, own, dims, preferred_element_type=F32)
        return kept, sent

    def exchange(x):
        return lax.all_to_all(x, "seq", split_axis=0, concat_axis=0, tiled=True)

    def after(x, *others):
        return lax.optimization_barrier((x, *others))[0]

    def joined(pair, *others):
        kept, sent = pair
        if sent is None:
            return kept
        return kept + after(sent, *others).astype(F32)

    nt = (((1,), (1,)), ((), ()))
    tn = (((0,), (0,)), ((), ()))
    seqs = range(seq_count)
    last = seq_count - 1
    full_out = lax.all_gather(out_weight.T, "seq", axis=0, tiled=True)
    full_in = lax.all_gather(in_weight, "seq", axis=0, tiled=True)

    sources = [inputs[s].reshape(blocks, size, chan) for s in seqs]
    cots = [cotangent[s] for s in seqs]
    cot_all = [gather_cols(c) for c in cots]

    turned = []
    for s in seqs:
        u = jnp.einsum("mkn,mnc->mkc", first_factor, sources[s], preferred_element_type=F32)
        u = u.astype(BF).reshape(blocks, owners, offs, chan).transpose(1, 0, 2, 3)
        if s > 0:
            u = after(u, cot_all[s - 1])
        turned.append(exchange(u).reshape(owners * blocks, offs, chan))
    dhs = [jnp.dot(cot_all[s], full_out, preferred_element_type=F32) for s in seqs]
    mixes, seconds, mixed_all = [], [], []
    for s in seqs:
        w = jnp.einsum("kjm,mkc->kjc", second_factor, turned[s], preferred_element_type=F32)
        w = w.astype(BF).reshape(offs, owners, blocks, chan).transpose(1, 0, 2, 3)
        if s == 0:
            w = after(w, cot_all[last])
        w = after(exchange(w), *(dhs if s == 0 else mixed_all))
        w = w.reshape(size, blocks, chan).transpose(1, 0, 2)
        w = lax.optimization_barrier(w)
        gate = jax.nn.sigmoid(gain * sources[s].astype(F32) + shift)
        seconds.append(w)
        mixes.append((gate * w.astype(F32)).astype(BF).reshape(tok_rows, chan))
        mixed_all.append(gather_cols(mixes[s]))

    das, hs, sums = [], [], []
    for s in seqs:
        pre = jnp.dot(mixed_all[s], full_in, preferred_element_type=F32)
        sig = jax.nn.sigmoid(pre)
        hs.append((pre * sig).astype(BF))
        das.append((dhs[s] * sig * (1.0 + pre * (1.0 - sig))).astype(BF))
        sums.append(reduce_cols(das[s], full_in, nt))
    dms, dws, gates, sends = [], [], [], []
    for s in seqs:
        gate = jax.nn.sigmoid(gain * sources[s].astype(F32) + shift)
        dm = cots[s].astype(F32) + joined(sums[s], das[last], *sends)
        dm = dm.astype(BF).reshape(blocks, size, chan)
        dw = (dm.astype(F32) * gate).astype(BF)
        dw = dw.reshape(blocks, owners, offs, chan).transpose(1, 0, 2, 3)
        dms.append(dm)
        gates.append(gate)
        sends.append(dw)
        dws.append(exchange(dw))
    hs[0] = after(hs[0], sends[0])
    out_term = sum(lax.dot_general(cot_all[s], hs[s], tn, preferred_element_type=F32) for s in seqs)
    in_term = sum(lax.dot_general(mixed_all[s], das[s], tn, preferred_element_type=F32) for s in seqs)
    out_term, in_term = out_term.astype(BF), in_term.astype(BF)
    scale = 1.0 / size
    grad_out = lax.psum_scatter(out_term, "seq", scatter_dimension=0, tiled=True)
    grad_in = lax.psum_scatter(in_term, "seq", scatter_dimension=0, tiled=True)

    dws[0] = after(dws[0], out_term, in_term)
    branches = [reduce_cols(hs[s], full_out, nt) for s in seqs]
    if groups == 2:
        dws[last] = after(dws[last], branches[0][1])
    grads, results = [], []
    for s in seqs:
        dw = dws[s].reshape(owners * blocks, offs, chan)
        du = jnp.einsum("kjm,jkc->kmc", second_factor, dw, preferred_element_type=F32)
        du = du.astype(BF).reshape(offs, owners, blocks, chan).transpose(1, 0, 2, 3)
        du = exchange(du)
        du, kept = lax.optimization_barrier((du, branches[s][0]))
        du = du.reshape(size, blocks, chan)
        back = jnp.einsum("mkn,kmc->mnc", first_factor, du, preferred_element_type=F32)
        gate = gates[s]
        gate_term = dms[s].astype(F32) * seconds[s].astype(F32) * gate * (1.0 - gate) * gain
        grads.append((back + gate_term).astype(BF).reshape(tok_rows, chan))
        branch = kept if branches[s][1] is None else kept + branches[s][1].astype(F32)
        results.append((mixes[s].astype(F32) + branch).astype(BF))
    return (
        jnp.stack(results),
        jnp.stack(grads),
        grad_in.astype(F32) * scale,
        grad_out.astype(F32).T * scale,
    )


def solution(mesh):
    in_specs = (
        P(None, "seq", "fsdp"),
        P("seq", None, None),
        P("seq", None, None),
        P("fsdp"),
        P("fsdp"),
        P("seq", "fsdp"),
        P("fsdp", "seq"),
        P(None, "seq", "fsdp"),
    )
    out_specs = (P(None, "seq", "fsdp"), P(None, "seq", "fsdp"), P("seq", "fsdp"), P("fsdp", "seq"))
    return jax.shard_map(body, mesh=mesh, in_specs=in_specs, out_specs=out_specs, check_vma=False)
```

```python
import jax
import jax.numpy as jnp
from jax import lax
from jax.sharding import PartitionSpec as P

BF = jnp.bfloat16
F32 = jnp.float32


def body(
    inputs, first_factor, second_factor, gate_scale, gate_bias, in_weight, out_weight, cotangent
):
    seq_count, tok_rows, chan = inputs.shape
    blocks, size, _ = first_factor.shape
    offs = second_factor.shape[0]
    owners = lax.axis_size("seq")
    groups = lax.axis_size("fsdp")
    mine = lax.axis_index("fsdp")
    width = chan * groups
    gain = gate_scale.reshape(1, 1, chan)
    shift = gate_bias.reshape(1, 1, chan)

    def swap(x):
        return lax.ppermute(x, "fsdp", [(0, 1), (1, 0)])

    def gather_cols(x):
        if groups != 2:
            return lax.all_gather(x, "fsdp", axis=1, tiled=True)
        return place(x, swap(x))

    def place(x, y):
        first = mine == 0
        return jnp.concatenate([jnp.where(first, x, y), jnp.where(first, y, x)], axis=1)

    def reduce_cols(left, weight, dims):
        if groups != 2:
            full = lax.dot_general(left, weight, dims, preferred_element_type=F32)
            got = lax.all_to_all(full, "fsdp", split_axis=1, concat_axis=0, tiled=True)
            return jnp.sum(got.reshape(groups, -1, chan), axis=0), None
        other = lax.dynamic_slice_in_dim(weight, (1 - mine) * chan, chan, 0)
        own = lax.dynamic_slice_in_dim(weight, mine * chan, chan, 0)
        sent = swap(lax.dot_general(left, other, dims, preferred_element_type=F32).astype(BF))
        kept = lax.dot_general(left, own, dims, preferred_element_type=F32)
        return kept, sent

    def exchange(x):
        return lax.all_to_all(x, "seq", split_axis=0, concat_axis=0, tiled=True)

    bar = lax.optimization_barrier
    nt = (((1,), (1,)), ((), ()))
    tn = (((0,), (0,)), ((), ()))
    seqs = range(seq_count)
    last = seq_count - 1
    both = jnp.stack([in_weight, out_weight.T], axis=0)
    both = lax.all_gather(both, "seq", axis=1, tiled=True)
    full_in, full_out = both[0], both[1]

    sources = [inputs[s].reshape(blocks, size, chan) for s in seqs]
    cots = [cotangent[s] for s in seqs]
    cot_all = [gather_cols(c) for c in cots]

    source = inputs.reshape(seq_count, blocks, size, chan)
    u = jnp.einsum("mkn,smnc->mksc", first_factor, source, preferred_element_type=F32)
    u = u.astype(BF).reshape(blocks, owners, offs, seq_count, chan).transpose(1, 3, 0, 2, 4)
    u, *cot_all = bar((exchange(u), *cot_all))
    turned = [u[:, s].reshape(owners * blocks, offs, chan) for s in seqs]
    mixes, seconds, mixed_all = [], [], []
    for s in seqs:
        w = jnp.einsum("kjm,mkc->kjc", second_factor, turned[s], preferred_element_type=F32)
        w = w.astype(BF).reshape(offs, owners, blocks, chan).transpose(1, 0, 2, 3)
        w = exchange(w)
        if s > 0:
            w, mixed_all[s - 1] = bar((w, mixed_all[s - 1]))
        w = bar(w.reshape(size, blocks, chan).transpose(1, 0, 2))
        gate = jax.nn.sigmoid(gain * sources[s].astype(F32) + shift)
        seconds.append(w)
        mixes.append((gate * w.astype(F32)).astype(BF).reshape(tok_rows, chan))
        if s < last or groups != 2:
            mixed_all.append(gather_cols(mixes[s]))
    swapped = swap(mixes[last]) if groups == 2 else None

    das, hs, sums = [], [], []
    for s in seqs:
        pre = jnp.dot(mixed_all[s], full_in, preferred_element_type=F32)
        dh = jnp.dot(cot_all[s], full_out, preferred_element_type=F32)
        sig = jax.nn.sigmoid(pre)
        hs.append((pre * sig).astype(BF))
        da = (dh * sig * (1.0 + pre * (1.0 - sig))).astype(BF)
        if s < last and groups == 2:
            da, swapped = bar((da, swapped))
            mixed_all.append(place(mixes[last], swapped))
        if s > 0 and groups == 2:
            kept, sent = sums[s - 1]
            da, sent = bar((da, sent))
            sums[s - 1] = kept, sent
        das.append(da)
        sums.append(reduce_cols(da, full_in, nt))

    out_term = sum(lax.dot_general(cot_all[s], hs[s], tn, preferred_element_type=F32) for s in seqs)
    out_term = out_term.astype(BF)
    if groups == 2:
        kept, sent = sums[last]
        sent, out_term = bar((sent, out_term))
        sums[last] = kept, sent
    grad_out = lax.psum_scatter(out_term, "seq", scatter_dimension=0, tiled=True)
    dms, dws, gates = [], [], []
    for s in seqs:
        gate = jax.nn.sigmoid(gain * sources[s].astype(F32) + shift)
        kept, sent = sums[s]
        dm = cots[s].astype(F32) + (kept if sent is None else kept + sent.astype(F32))
        dm = dm.astype(BF).reshape(blocks, size, chan)
        dw = (dm.astype(F32) * gate).astype(BF)
        dms.append(dm)
        gates.append(gate)
        dws.append(dw.reshape(blocks, owners, offs, chan).transpose(1, 0, 2, 3))
    dw = exchange(jnp.stack(dws, axis=1))
    in_term = sum(lax.dot_general(mixed_all[s], das[s], tn, preferred_element_type=F32) for s in seqs)
    dw, in_term = bar((dw, in_term.astype(BF)))
    scale = 1.0 / size
    grad_in = lax.psum_scatter(in_term, "seq", scatter_dimension=0, tiled=True)

    branches = [list(reduce_cols(hs[s], full_out, nt)) for s in seqs]
    dw = dw.transpose(1, 0, 2, 3, 4).reshape(seq_count, owners * blocks, offs, chan)
    du = jnp.einsum("kjm,sjkc->kmsc", second_factor, dw, preferred_element_type=F32)
    du = du.astype(BF).reshape(offs, owners, blocks, seq_count, chan).transpose(1, 3, 0, 2, 4)
    du = exchange(du)
    if groups == 2:
        du, *sents = bar((du, *[pair[1] for pair in branches]))
        branches = [[pair[0], sent] for pair, sent in zip(branches, sents)]
    grads, results = [], []
    for s in seqs:
        rows = du[:, s].reshape(size, blocks, chan)
        back = jnp.einsum("mkn,kmc->mnc", first_factor, rows, preferred_element_type=F32)
        gate = gates[s]
        gate_term = dms[s].astype(F32) * seconds[s].astype(F32) * gate * (1.0 - gate) * gain
        grads.append((back + gate_term).astype(BF).reshape(tok_rows, chan))
        kept, sent = branches[s]
        branch = kept if sent is None else kept + sent.astype(F32)
        results.append((mixes[s].astype(F32) + branch).astype(BF))
    return (
        jnp.stack(results),
        jnp.stack(grads),
        grad_in.astype(F32) * scale,
        grad_out.astype(F32).T * scale,
    )


def solution(mesh):
    in_specs = (
        P(None, "seq", "fsdp"),
        P("seq", None, None),
        P("seq", None, None),
        P("fsdp"),
        P("fsdp"),
        P("seq", "fsdp"),
        P("fsdp", "seq"),
        P(None, "seq", "fsdp"),
    )
    out_specs = (P(None, "seq", "fsdp"), P(None, "seq", "fsdp"), P("seq", "fsdp"), P("fsdp", "seq"))
    return jax.shard_map(body, mesh=mesh, in_specs=in_specs, out_specs=out_specs, check_vma=False)
```
